32 devices in a mesh: groups: 2 (over y), snap: 4 (over z), slab: 2 (over x), sub: 2 (over core).
Axes of the slice: x: 2, y: 2, z: 4, core: 2. Of those that a mesh axis runs over, the one named last changes fastest.
Arguments:
- fields: float32 [8, 4, 4, 16, 128], P(('groups', 'snap'), None, 'slab', 'sub'), parts along dimension 0, may hold values from -18 to 18
- snap_ids: int32 [8], P(('groups', 'snap')), parts along dimension 0, may hold values from 0 to 63
- snap_weight: float32 [64], replicated, may hold values from 0.5 to 2
- product_terms: int32 [192, 3], replicated, may hold values from 0 to 27, as said below
- mix_weight: float32 [192], replicated, may hold values from -1.5 to 1.5
Outputs:
- whitened: bfloat16 [8, 192, 4, 16, 128], P(('groups', 'snap'), None, 'slab', 'sub'), parts along dimension 0
- r_factor: float32 [384, 192], P('groups'), parts along dimension 0
The draws below stay inside these ranges and needn't reach their ends.
There are 2 independent parts, one for each index of `groups`. The reference program is written for one: setup_inputs(seed, part) draws one part's arguments, and reference() takes and returns one part's arrays. A program takes and returns all parts, laid end to end along the dimension named above; an argument that names none is the same for every part. Nothing has to cross between parts.
Inputs may be any that keep to these rules, and one draw needn't show every extreme that they name: `product_terms`: each row names three different bases, and no two rows are equal.
All inputs are finite; a program needn't handle non-finite values.
Results may differ from the reference program's by a relative error of at most 0.0028.
Values sent between devices are 32-bit elements; how exact they have to be, the bound alone decides.
A program may use at most 64 MiB of HBM per device.

```python
import math
import jax
import jax.numpy as jnp
from jax import lax

NY = 128
NFEAT = 192
NBASE = 28
TABLE = 64
SNAPS = 4
NZ = 4
NX = 16
CELLS = 32768


def draw_fields(key, part):
    shape = (SNAPS, 4, NZ, NX, NY)
    ramp = 1.0 + 2.0 * jnp.arange(SNAPS, dtype=jnp.float32) / max(SNAPS - 1, 1)
    ramp = ramp[:, None, None, None, None]
    values = ramp * jnp.clip(jax.random.normal(key, shape, jnp.float32), -6.0, 6.0)
    return values


def draw_product_terms(key, part):
    count_all = NBASE * (NBASE - 1) * (NBASE - 2)
    codes = jax.random.permutation(key, count_all)[:NFEAT].astype(jnp.int32)
    span_inner = (NBASE - 1) * (NBASE - 2)
    first_index = codes // span_inner
    remain = codes % span_inner
    second_raw = remain // (NBASE - 2)
    third_raw = remain % (NBASE - 2)
    second_index = second_raw + (second_raw >= first_index).astype(jnp.int32)
    lower_index = jnp.minimum(first_index, second_index)
    upper_index = jnp.maximum(first_index, second_index)
    third_index = third_raw + (third_raw >= lower_index).astype(jnp.int32)
    third_index = third_index + (third_index >= upper_index).astype(jnp.int32)
    return jnp.stack([first_index, second_index, third_index], axis=1).astype(jnp.int32)


def with_ends(drawn, key, low, top_value):
    longest = drawn.shape.index(max(drawn.shape))
    spots = []
    for shift in (0, 1):
        where = [jax.random.randint(jax.random.fold_in(key, axis), (), 0, length) for axis, length in enumerate(drawn.shape)]
        where[longest] = (where[longest] + shift) % drawn.shape[longest]
        spots.append(tuple(where))
    return drawn.at[spots[0]].set(low).at[spots[1]].set(top_value)


def setup_inputs(seed: int = 0, part: int = 0) -> dict:
    keys = jax.random.split(jax.random.key(seed), 6)
    part_keys = jax.random.split(jax.random.fold_in(keys[5], part), 6)
    return {
        "fields": draw_fields(jax.random.fold_in(jax.random.fold_in(keys[5], part), 71), part),
        "snap_ids": with_ends(jax.random.randint(part_keys[1], (SNAPS,), 0, TABLE), jax.random.fold_in(part_keys[1], 1), 0, TABLE - 1).astype(jnp.int32),
        "snap_weight": jnp.clip(jnp.exp(jax.random.uniform(keys[2], (TABLE,), jnp.float32, math.log(0.5), math.log(2.0))), 0.5, 2.0),
        "product_terms": draw_product_terms(jax.random.fold_in(keys[5], 71), part),
        "mix_weight": jnp.clip(jax.random.uniform(keys[4], (NFEAT,), jnp.float32, -1.5, 1.5), -1.5, 1.5),
    }


ridge_value = 0.05

def stencil_pair(values, along):
    ahead_one = jnp.roll(values, -1, along)
    behind_one = jnp.roll(values, 1, along)
    ahead_two = jnp.roll(values, -2, along)
    behind_two = jnp.roll(values, 2, along)
    first_deriv = (8.0 * (ahead_one - behind_one) - (ahead_two - behind_two)) / 12.0
    second_deriv = (16.0 * (ahead_one + behind_one) - (ahead_two + behind_two) - 30.0 * values) / 12.0
    return (first_deriv, second_deriv)

def snapshot_features(field_block, snap_scale, product_terms, mix_weight):
    z_first, z_second = stencil_pair(field_block, 1)
    x_first, x_second = stencil_pair(field_block, 2)
    y_first, y_second = stencil_pair(field_block, 3)
    stacked = jnp.stack([field_block, z_first, x_first, y_first, z_second, x_second, y_second], axis=1)
    bases = stacked.reshape(NBASE, -1)
    left_term = bases[product_terms[:, 0]]
    middle = bases[product_terms[:, 1]]
    right_term = bases[product_terms[:, 2]]
    return snap_scale * left_term * (middle + mix_weight[:, None] * right_term)

def reference(fields, snap_ids, snap_weight, product_terms, mix_weight):
    scales = snap_weight[snap_ids.astype(jnp.int32)]

    def accumulate(total_gram, snapshot):
        field_block, snap_scale = snapshot
        features = snapshot_features(field_block, snap_scale, product_terms, mix_weight)
        product = lax.dot_general(features, features, (((1,), (1,)), ((), ())), precision=lax.Precision.HIGHEST)
        return (total_gram + product, None)
    total_gram, _ = lax.scan(accumulate, jnp.zeros((NFEAT, NFEAT), jnp.float32), (fields, scales))
    gram = total_gram / CELLS + ridge_value * jnp.eye(NFEAT, dtype=jnp.float32)
    r_factor = jnp.linalg.cholesky(gram).T

    def whiten(snapshot):
        field_block, snap_scale = snapshot
        features = snapshot_features(field_block, snap_scale, product_terms, mix_weight)
        solved = jax.scipy.linalg.solve_triangular(r_factor, features, trans=1, lower=False)
        return solved.reshape(NFEAT, NZ, NX, NY).astype(jnp.bfloat16)
    whitened = lax.map(whiten, (fields, scales))
    return (whitened, r_factor)
```

```python
import jax
import jax.numpy as jnp
from jax import lax
from jax.experimental import pallas as pl
from jax.experimental.pallas import tpu as pltpu
from jax.sharding import PartitionSpec as P

ridge_value = 0.05
panel_rows = 32
HIGHEST = lax.Precision.HIGHEST


def padded_2(block, sides, width):
    for axis, dim in sides:
        count = lax.axis_size(axis)
        forward = [(i, i + 1) for i in range(count - 1)]
        forward.append((count - 1, 0))
        backward = [(target, source) for source, target in forward]
        low = lax.ppermute(
            lax.slice_in_dim(block, block.shape[dim] - width, None, axis=dim), axis, forward
        )
        high = lax.ppermute(lax.slice_in_dim(block, 0, width, axis=dim), axis, backward)
        block = jnp.concatenate([low, block, high], axis=dim)
    return block


def stencil_pair(values, ahead_one, behind_one, ahead_two, behind_two):
    first_deriv = (8.0 * (ahead_one - behind_one) - (ahead_two - behind_two)) / 12.0
    second_deriv = (
        16.0 * (ahead_one + behind_one) - (ahead_two + behind_two) - 30.0 * values
    ) / 12.0
    return (first_deriv, second_deriv)


def dot_highest(left_matrix, right_matrix):
    return jnp.dot(left_matrix, right_matrix, precision=HIGHEST)


def eliminate(work, order):
    half = work.shape[1] // 2
    for start in range(0, order, panel_rows):
        stop = start + panel_rows
        low = start // 128 * 128
        high = half + (stop + 127) // 128 * 128
        panel = work[start:stop, low:high]
        row_index = lax.broadcasted_iota(jnp.int32, (panel_rows, 1), 0)
        pivots = jnp.ones((panel_rows, 1), jnp.float32)
        for step in range(panel_rows):
            place = start + step - low
            row = panel[step : step + 1, :]
            pivot = panel[step : step + 1, place : place + 1]
            pivots = jnp.where(row_index == step, pivot, pivots)
            if step + 1 < panel_rows:
                column = panel[:, place : place + 1] * (1.0 / pivot)
                panel = panel - jnp.where(row_index > step, column, 0.0) * row
        panel = panel * (1.0 / jnp.sqrt(pivots))
        work[start:stop, low:high] = panel
        if stop < order:
            sides = panel[:, : half - low].T[stop - low : order - low, :]
            work[stop:order, low:high] = work[stop:order, low:high] - jnp.dot(
                sides, panel, precision=HIGHEST, preferred_element_type=jnp.float32
            )


def whiten_kernel(cells_total, gram_ref, feature_ref, white_ref, factor_ref, work, spread):
    order = gram_ref.shape[0]
    half = work.shape[1] // 2
    rows = lax.broadcasted_iota(jnp.int32, (order, order), 0)
    columns = lax.broadcasted_iota(jnp.int32, (order, order), 1)
    identity = (rows == columns).astype(jnp.float32)
    work[...] = jnp.zeros_like(work)
    work[:, :order] = gram_ref[...] * (1.0 / cells_total) + ridge_value * identity
    work[:, half : half + order] = identity
    eliminate(work, order)
    factor_ref[...] = jnp.where(columns >= rows, work[:, :order], 0.0)
    inverse = jnp.where(columns <= rows, work[:, half : half + order], 0.0)
    tiles = feature_ref.shape[1] // 128
    for tile in range(0, tiles, 2):
        solved = jnp.dot(
            inverse,
            feature_ref[:, tile * 128 : tile * 128 + 256],
            precision=HIGHEST,
            preferred_element_type=jnp.float32,
        )
        spread[pl.ds(tile, order, stride=tiles), :] = solved[:, :128]
        spread[pl.ds(tile + 1, order, stride=tiles), :] = solved[:, 128:]
    white_ref[...] = spread[...].reshape(white_ref.shape).astype(white_ref.dtype)


def local(fields, snap_ids, snap_weight, product_terms, mix_weight):
    padded = padded_2(fields, (("slab", 2), ("sub", 3)), 2)
    layers = fields.shape[2]
    columns = fields.shape[3]
    center = padded[0, :, 2 : 2 + layers, 2 : 2 + columns, :]

    def along_z(offset):
        return padded[0, :, 2 + offset : 2 + offset + layers, 2 : 2 + columns, :]

    def along_x(offset):
        return padded[0, :, 2 : 2 + layers, 2 + offset : 2 + offset + columns, :]

    z_first, z_second = stencil_pair(center, along_z(1), along_z(-1), along_z(2), along_z(-2))
    x_first, x_second = stencil_pair(center, along_x(1), along_x(-1), along_x(2), along_x(-2))
    y_first, y_second = stencil_pair(
        center,
        jnp.roll(center, -1, 3),
        jnp.roll(center, 1, 3),
        jnp.roll(center, -2, 3),
        jnp.roll(center, 2, 3),
    )
    stacked = jnp.stack([center, z_first, x_first, y_first, z_second, x_second, y_second], axis=1)
    base_count = stacked.shape[0] * stacked.shape[1]
    bases = stacked.reshape(base_count, -1)
    table_size = snap_weight.shape[0]
    snap_scale = jnp.sum(jnp.where(jnp.arange(table_size) == snap_ids[0], snap_weight, 0.0))
    feature_count = product_terms.shape[0]
    choose = (product_terms.T.reshape(-1)[:, None] == jnp.arange(base_count)[None, :]).astype(
        jnp.float32
    )
    picked = dot_highest(choose, bases)
    left_term = picked[:feature_count]
    middle = picked[feature_count : 2 * feature_count]
    right_term = picked[2 * feature_count :]
    features = snap_scale * left_term * (middle + mix_weight[:, None] * right_term)
    local_gram = lax.dot_general(
        features, features, (((1,), (1,)), ((), ())), precision=HIGHEST
    )
    cells = bases.shape[1]
    cells_total = float(
        lax.axis_size("snap") * lax.axis_size("slab") * lax.axis_size("sub") * cells
    )
    total_gram = lax.psum(local_gram, ("snap", "slab", "sub"))
    import functools

    whitened, r_factor = pl.pallas_call(
        functools.partial(whiten_kernel, cells_total),
        out_shape=(
            jax.ShapeDtypeStruct((1, feature_count, layers, columns, fields.shape[4]), jnp.bfloat16),
            jax.ShapeDtypeStruct((feature_count, feature_count), jnp.float32),
        ),
        in_specs=[pl.BlockSpec(memory_space=pltpu.VMEM)] * 2,
        out_specs=(pl.BlockSpec(memory_space=pltpu.VMEM),) * 2,
        scratch_shapes=[
            pltpu.VMEM((feature_count, 512), jnp.float32),
            pltpu.VMEM((feature_count * (cells // 128), 128), jnp.float32),
        ],
    )(total_gram, features)
    return (whitened, r_factor)


def solution(mesh):
    return jax.shard_map(
        local,
        mesh=mesh,
        in_specs=(
            P(("groups", "snap"), None, "slab", "sub", None),
            P(("groups", "snap")),
            P(),
            P(),
            P(),
        ),
        out_specs=(P(("groups", "snap"), None, "slab", "sub", None), P("groups", None)),
        check_vma=False,
    )
```

```python
import functools

import jax
import jax.numpy as jnp
from jax import lax
from jax.experimental import pallas as pl
from jax.experimental.pallas import tpu as pltpu
from jax.sharding import PartitionSpec as P

ridge_value = 0.05
panel_rows = 32
HIGHEST = lax.Precision.HIGHEST
MESH = pl.DeviceIdType.MESH


def eliminate(work, order):
    half = work.shape[1] // 2
    for start in range(0, order, panel_rows):
        stop = start + panel_rows
        low = start // 128 * 128
        high = half + (stop + 127) // 128 * 128
        panel = work[start:stop, low:high]
        row_index = lax.broadcasted_iota(jnp.int32, (panel_rows, 1), 0)
        pivots = jnp.ones((panel_rows, 1), jnp.float32)
        for step in range(panel_rows):
            place = start + step - low
            row = panel[step : step + 1, :]
            pivot = panel[step : step + 1, place : place + 1]
            pivots = jnp.where(row_index == step, pivot, pivots)
            if step + 1 < panel_rows:
                column = panel[:, place : place + 1] * (1.0 / pivot)
                panel = panel - jnp.where(row_index > step, column, 0.0) * row
        panel = panel * (1.0 / jnp.sqrt(pivots))
        work[start:stop, low:high] = panel
        if stop < order:
            sides = panel[:, : half - low].T[stop - low : order - low, :]
            work[stop:order, low:high] = work[stop:order, low:high] - jnp.dot(
                sides, panel, precision=HIGHEST, preferred_element_type=jnp.float32
            )


def whiten_kernel(cells_total, gram_ref, feature_ref, white_ref, factor_ref, work, spread):
    order = gram_ref.shape[0]
    half = work.shape[1] // 2
    rows = lax.broadcasted_iota(jnp.int32, (order, order), 0)
    columns = lax.broadcasted_iota(jnp.int32, (order, order), 1)
    identity = (rows == columns).astype(jnp.float32)
    work[...] = jnp.zeros_like(work)
    work[:, :order] = gram_ref[...] * (1.0 / cells_total) + ridge_value * identity
    work[:, half : half + order] = identity
    eliminate(work, order)
    factor_ref[...] = jnp.where(columns >= rows, work[:, :order], 0.0)
    inverse = jnp.where(columns <= rows, work[:, half : half + order], 0.0)
    tiles = feature_ref.shape[1] // 128
    for tile in range(0, tiles, 2):
        solved = jnp.dot(
            inverse,
            feature_ref[:, tile * 128 : tile * 128 + 256],
            precision=HIGHEST,
            preferred_element_type=jnp.float32,
        )
        spread[pl.ds(tile, order, stride=tiles), :] = solved[:, :128]
        spread[pl.ds(tile + 1, order, stride=tiles), :] = solved[:, 128:]
    white_ref[...] = spread[...].reshape(white_ref.shape).astype(white_ref.dtype)


def plane_device(place, subs):
    return {"slab": lax.div(place, subs), "sub": lax.rem(place, subs)}


def gram_kernel(
    counts,
    fields_ref,
    ids_ref,
    weight_ref,
    terms_ref,
    mix_ref,
    gram_ref,
    feature_ref,
    halo_z,
    halo_x,
    natural,
    partial,
    landed,
    snaps_sum,
    total,
    halo_send,
    halo_recv,
    plane_send,
    plane_recv,
    snap_send,
    snap_recv,
    gather_send,
    gather_recv,
):
    slabs, subs, snaps = counts
    plane = slabs * subs
    slab, sub, snap = lax.axis_index("slab"), lax.axis_index("sub"), lax.axis_index("snap")
    me = slab * subs + sub
    plane_peers = [plane_device(lax.rem(me + k, plane), subs) for k in range(1, plane)]
    snap_peers = [{"snap": lax.rem(snap + k, snaps)} for k in range(1, snaps)]

    barrier = pltpu.get_barrier_semaphore()
    for peer in plane_peers + snap_peers:
        pl.semaphore_signal(barrier, inc=1, device_id=peer, device_id_type=MESH)
    pl.semaphore_wait(barrier, len(plane_peers) + len(snap_peers))

    copies = []
    for axis, index, count, halo, base in (
        ("slab", slab, slabs, halo_z, 0),
        ("sub", sub, subs, halo_x, 2),
    ):
        for side, move in ((0, 1), (1, count - 1))[: 1 if count == 2 else 2]:
            copy = pltpu.make_async_remote_copy(
                src_ref=fields_ref.at[0],
                dst_ref=halo.at[side],
                send_sem=halo_send.at[base + side],
                recv_sem=halo_recv.at[base + side],
                device_id={axis: lax.rem(index + move, count)},
                device_id_type=MESH,
            )
            copy.start()
            copies.append(copy)

    features, terms = terms_ref.shape
    field_count, layers, columns, width = fields_ref.shape[1:]
    cells_rows = layers * columns
    row_of = lax.broadcasted_iota(jnp.int32, (features, 96), 1)
    base_of = lax.rem(row_of, 32)
    chosen = [
        (terms_ref[:, k : k + 1] == base_of).astype(jnp.float32).astype(jnp.bfloat16)
        for k in range(3)
    ]
    choose = jnp.concatenate(chosen, axis=0)
    table = lax.broadcasted_iota(jnp.int32, weight_ref.shape, 1)
    scale = jnp.sum(
        jnp.where(table == ids_ref[0], weight_ref[...], 0.0), axis=1, keepdims=True
    )
    square_rows = lax.broadcasted_iota(jnp.int32, (features, features), 0)
    square_columns = lax.broadcasted_iota(jnp.int32, (features, features), 1)
    mix = jnp.sum(
        jnp.where(square_rows == square_columns, mix_ref[...], 0.0), axis=1, keepdims=True
    )
    natural[28 * cells_rows :, :] = jnp.zeros((4 * cells_rows, width), jnp.float32)

    def put(field, kind, layer, tile):
        start = (field * 7 + kind) * cells_rows + layer * columns
        natural[start : start + columns, :] = tile

    def pair(center, ahead_one, behind_one, ahead_two, behind_two):
        first = 8.0 * (ahead_one - behind_one) - (ahead_two - behind_two)
        second = 16.0 * (ahead_one + behind_one) - (ahead_two + behind_two) - 30.0 * center
        return first * (1.0 / 12.0), second * (1.0 / 12.0)

    for f in range(field_count):
        for z in range(layers):
            tile = fields_ref[0, f, z]
            put(f, 0, z, tile)
            y_shifts = [pltpu.roll(tile, s % width, 1) for s in (-1, 1, -2, 2)]
            first, second = pair(tile, *y_shifts)
            put(f, 3, z, first)
            put(f, 6, z, second)

    for copy in copies:
        copy.wait()

    z_low, z_high = 0, 0 if slabs == 2 else 1
    x_low, x_high = 0, 0 if subs == 2 else 1
    line = lax.broadcasted_iota(jnp.int32, (columns, width), 0)
    for f in range(field_count):
        column = [halo_z[z_low, f, z] for z in range(layers)]
        column += [fields_ref[0, f, z] for z in range(layers)]
        column += [halo_z[z_high, f, z] for z in range(layers)]
        for z in range(layers):
            tile = column[layers + z]
            at = layers + z
            first, second = pair(
                tile, column[at + 1], column[at - 1], column[at + 2], column[at - 2]
            )
            put(f, 1, z, first)
            put(f, 4, z, second)
            low, high = halo_x[x_low, f, z], halo_x[x_high, f, z]
            shifts = []
            for s in (-1, 1, -2, 2):
                turned = pltpu.roll(tile, s % columns, 0)
                other = pltpu.roll(high if s < 0 else low, s % columns, 0)
                inside = line < columns + s if s < 0 else line >= s
                shifts.append(jnp.where(inside, turned, other))
            first, second = pair(tile, *shifts)
            put(f, 2, z, first)
            put(f, 5, z, second)

    for start in range(0, cells_rows, 2):
        pieces = []
        for at in (start, start + 1):
            whole = natural[pl.ds(at, 32, stride=cells_rows), :]
            upper = whole.astype(jnp.bfloat16)
            rest = whole - upper.astype(jnp.float32)
            centre = rest.astype(jnp.bfloat16)
            lower = (rest - centre.astype(jnp.float32)).astype(jnp.bfloat16)
            pieces.append(jnp.concatenate([upper, centre, lower], axis=0))
        picked = jnp.dot(
            choose, jnp.concatenate(pieces, axis=1), preferred_element_type=jnp.float32
        )
        left, middle = picked[:features], picked[features : 2 * features]
        right = picked[2 * features :]
        feature_ref[:, start * width : (start + 2) * width] = (
            scale * left * (middle + mix * right)
        )

    everything = feature_ref[...]
    gram = lax.dot_general(
        everything,
        everything,
        (((1,), (1,)), ((), ())),
        precision=HIGHEST,
        preferred_element_type=jnp.float32,
    )
    rows = features // plane
    for k in range(plane):
        partial[k] = gram[k * rows : (k + 1) * rows, :]

    copies = []
    for k in range(1, plane):
        copy = pltpu.make_async_remote_copy(
            src_ref=partial.at[lax.rem(me + k, plane)],
            dst_ref=landed.at[k - 1],
            send_sem=plane_send.at[k - 1],
            recv_sem=plane_recv.at[k - 1],
            device_id=plane_peers[k - 1],
            device_id_type=MESH,
        )
        copy.start()
        copies.append(copy)
    block = partial[me]
    for k in range(1, plane):
        copies[k - 1].wait()
        block = block + landed[k - 1]
    snaps_sum[snap] = block

    copies = []
    for k in range(1, snaps):
        copy = pltpu.make_async_remote_copy(
            src_ref=snaps_sum.at[snap],
            dst_ref=snaps_sum.at[snap],
            send_sem=snap_send.at[k - 1],
            recv_sem=snap_recv.at[k - 1],
            device_id=snap_peers[k - 1],
            device_id_type=MESH,
        )
        copy.start()
        copies.append(copy)
    for copy in copies:
        copy.wait()
    block = snaps_sum[0]
    for k in range(1, snaps):
        block = block + snaps_sum[k]
    total[me] = block

    copies = []
    for k in range(1, plane):
        copy = pltpu.make_async_remote_copy(
            src_ref=total.at[me],
            dst_ref=total.at[me],
            send_sem=gather_send.at[k - 1],
            recv_sem=gather_recv.at[k - 1],
            device_id=plane_peers[k - 1],
            device_id_type=MESH,
        )
        copy.start()
        copies.append(copy)
    for copy in copies:
        copy.wait()
    for k in range(plane):
        gram_ref[k * rows : (k + 1) * rows, :] = total[k]


def local(fields, snap_ids, snap_weight, product_terms, mix_weight):
    counts = tuple(lax.axis_size(axis) for axis in ("slab", "sub", "snap"))
    slabs, subs, snaps = counts
    plane = slabs * subs
    field_count, layers, columns, width = fields.shape[1:]
    features = product_terms.shape[0]
    cells = layers * columns * width
    rows = features // plane
    f32 = jnp.float32
    in_vmem = pl.BlockSpec(memory_space=pltpu.VMEM)
    total_gram, values = pl.pallas_call(
        functools.partial(gram_kernel, counts),
        out_shape=(
            jax.ShapeDtypeStruct((features, features), f32),
            jax.ShapeDtypeStruct((features, cells), f32),
        ),
        in_specs=[in_vmem, pl.BlockSpec(memory_space=pltpu.SMEM), in_vmem, in_vmem, in_vmem],
        out_specs=(in_vmem, in_vmem),
        scratch_shapes=[
            pltpu.VMEM((2,) + fields.shape[1:], f32),
            pltpu.VMEM((2,) + fields.shape[1:], f32),
            pltpu.VMEM((32 * layers * columns, width), f32),
            pltpu.VMEM((plane, rows, features), f32),
            pltpu.VMEM((plane - 1, rows, features), f32),
            pltpu.VMEM((snaps, rows, features), f32),
            pltpu.VMEM((plane, rows, features), f32),
            pltpu.SemaphoreType.DMA((4,)),
            pltpu.SemaphoreType.DMA((4,)),
            pltpu.SemaphoreType.DMA((plane - 1,)),
            pltpu.SemaphoreType.DMA((plane - 1,)),
            pltpu.SemaphoreType.DMA((snaps - 1,)),
            pltpu.SemaphoreType.DMA((snaps - 1,)),
            pltpu.SemaphoreType.DMA((plane - 1,)),
            pltpu.SemaphoreType.DMA((plane - 1,)),
        ],
        compiler_params=pltpu.CompilerParams(collective_id=0, has_side_effects=True),
    )(fields, snap_ids, snap_weight.reshape(1, -1), product_terms, mix_weight.reshape(1, -1))
    whitened, r_factor = pl.pallas_call(
        functools.partial(whiten_kernel, float(snaps * plane * cells)),
        out_shape=(
            jax.ShapeDtypeStruct((1, features, layers, columns, width), jnp.bfloat16),
            jax.ShapeDtypeStruct((features, features), f32),
        ),
        in_specs=[in_vmem, in_vmem],
        out_specs=(in_vmem, in_vmem),
        scratch_shapes=[
            pltpu.VMEM((features, 512), f32),
            pltpu.VMEM((features * (cells // 128), 128), f32),
        ],
    )(total_gram, values)
    return (whitened, r_factor)


def solution(mesh):
    return jax.shard_map(
        local,
        mesh=mesh,
        in_specs=(
            P(("groups", "snap"), None, "slab", "sub", None),
            P(("groups", "snap")),
            P(),
            P(),
            P(),
        ),
        out_specs=(P(("groups", "snap"), None, "slab", "sub", None), P("groups", None)),
        check_vma=False,
    )
```

```python
import functools

import jax
import jax.numpy as jnp
from jax import lax
from jax.experimental import pallas as pl
from jax.experimental.pallas import tpu as pltpu
from jax.sharding import PartitionSpec as P

ridge_value = 0.05
panel_rows = 32
HIGHEST = lax.Precision.HIGHEST
MESH = pl.DeviceIdType.MESH


def split(values, count):
    parts = []
    for _ in range(count):
        part = values.astype(jnp.bfloat16)
        parts.append(part)
        values = values - part.astype(jnp.float32)
    return parts


def row_of(tile, place):
    return jnp.broadcast_to(tile[place : place + 1, :], tile.shape)


def eliminate_group(groups, first, place):
    line = lax.broadcasted_iota(jnp.int32, (8, 128), 0)
    lane_tile, lane = place // 128, place % 128
    later = range(first, len(groups))
    spread = {
        (r, c): jnp.broadcast_to(
            groups[r][lane_tile][:, lane + c : lane + c + 1], (8, 128)
        )
        for r in later
        for c in range(8)
    }
    pivots = jnp.ones((8, 128), jnp.float32)
    factors = []
    for j in range(8):
        pivot = row_of(spread[first, j], j)
        pivots = jnp.where(line == j, pivot, pivots)
        inverse = 1.0 / pivot
        scaled = {r: spread[r, j] * inverse for r in later}
        scaled[first] = jnp.where(line > j, scaled[first], 0.0)
        factors.append(scaled)
        for c in range(j + 1, 8):
            head = row_of(spread[first, c], j)
            for r in later:
                spread[r, c] = spread[r, c] - scaled[r] * head
    for t in range(len(groups[first])):
        tile = groups[first][t]
        for j in range(8):
            head = row_of(tile, j)
            if j < 7:
                tile = tile - factors[j][first] * head
            for r in later:
                if r > first:
                    groups[r][t] = groups[r][t] - factors[j][r] * head
        groups[first][t] = tile
    return 1.0 / jnp.sqrt(pivots)


def eliminate(work, order):
    half = work.shape[1] // 2
    for start in range(0, order, panel_rows):
        stop = start + panel_rows
        low = start // 128 * 128
        high = half + (stop + 127) // 128 * 128
        tiles = (high - low) // 128
        groups = [
            [work[r : r + 8, low + 128 * t : low + 128 * t + 128] for t in range(tiles)]
            for r in range(start, stop, 8)
        ]
        scales = [
            eliminate_group(groups, g, start + 8 * g - low) for g in range(panel_rows // 8)
        ]
        rows = [
            jnp.concatenate([tile * scale for tile in group], axis=1)
            for group, scale in zip(groups, scales)
        ]
        panel = jnp.concatenate(rows, axis=0)
        work[start:stop, low:high] = panel
        if stop < order:
            sides = panel[:, : half - low].T[stop - low : order - low, :]
            a, b, c = split(sides, 3)
            d, e, f = split(panel, 3)
            left = jnp.concatenate([a, a, b, b, a, c], axis=1)
            right = jnp.concatenate([d, e, d, e, f, d], axis=0)
            work[stop:order, low:high] = work[stop:order, low:high] - jnp.dot(
                left, right, preferred_element_type=jnp.float32
            )


def whiten_kernel(
    cells_total, packed_ref, feature_in, white_ref, factor_ref, work, spread, feature_ref, done
):
    feature_copy = pltpu.make_async_copy(feature_in, feature_ref, done)
    feature_copy.start()
    order = factor_ref.shape[0]
    middle = packed_ref.shape[0]
    half = work.shape[1] // 2
    rows = lax.broadcasted_iota(jnp.int32, (order, order), 0)
    columns = lax.broadcasted_iota(jnp.int32, (order, order), 1)
    row = lax.broadcasted_iota(jnp.int32, (middle, 128), 0)
    lane = lax.broadcasted_iota(jnp.int32, (middle, 128), 1)
    left = packed_ref[:, :128]
    turned = jnp.concatenate([left, jnp.zeros((128 - middle, 128), jnp.float32)], axis=0).T
    turned = turned[:middle, :]
    work[:middle, :128] = jnp.where((lane >= row) | (lane >= middle), left, turned)
    work[:middle, 128:half] = jnp.where(lane + 128 < order, packed_ref[:, 128:], 0.0)
    corner = packed_ref[:, order : order + 1]
    lower = jnp.where(lane < row, left, jnp.where(lane > row, turned, corner))
    lower = jnp.where(lane < middle, lower, 0.0)
    lower = jnp.concatenate([lower, jnp.zeros((middle, half - 128), jnp.float32)], axis=1)
    work[middle:, :half] = pltpu.roll(lower, middle, 1)
    long_rows = lax.broadcasted_iota(jnp.int32, (order, half), 0)
    long_columns = lax.broadcasted_iota(jnp.int32, (order, half), 1)
    identity = (long_rows == long_columns).astype(jnp.float32)
    work[:, half:] = identity
    work[:, :half] = work[:, :half] * (1.0 / cells_total) + ridge_value * identity
    eliminate(work, order)
    factor_ref[...] = jnp.where(columns >= rows, work[:, :order], 0.0)
    inverse = jnp.where(columns <= rows, work[:, half : half + order], 0.0)
    upper, lower = split(inverse, 2)
    feature_copy.wait()
    tiles = feature_ref.shape[1] // 128
    for tile in range(0, tiles, 2):
        first, second = split(feature_ref[:, tile * 128 : tile * 128 + 256], 2)
        solved = (
            jnp.dot(upper, first, preferred_element_type=jnp.float32)
            + jnp.dot(upper, second, preferred_element_type=jnp.float32)
            + jnp.dot(lower, first, preferred_element_type=jnp.float32)
        )
        spread[pl.ds(tile, order, stride=tiles), :] = solved[:, :128]
        spread[pl.ds(tile + 1, order, stride=tiles), :] = solved[:, 128:]
    white_ref[...] = spread[...].reshape(white_ref.shape).astype(white_ref.dtype)


def plane_device(place, subs):
    return {"slab": lax.div(place, subs), "sub": lax.rem(place, subs)}


def gram_kernel(
    counts,
    fields_ref,
    ids_ref,
    weight_ref,
    terms_ref,
    mix_ref,
    packed_ref,
    feature_out,
    feature_ref,
    gram_wide,
    feature_done,
    halo_z,
    halo_x,
    natural,
    partial,
    landed,
    snaps_sum,
    total,
    halo_send,
    halo_recv,
    plane_send,
    plane_recv,
    snap_send,
    snap_recv,
    gather_send,
    gather_recv,
):
    slabs, subs, snaps = counts
    plane = slabs * subs
    slab, sub, snap = lax.axis_index("slab"), lax.axis_index("sub"), lax.axis_index("snap")
    me = slab * subs + sub
    plane_peers = [plane_device(lax.rem(me + k, plane), subs) for k in range(1, plane)]
    snap_peers = [{"snap": lax.rem(snap + k, snaps)} for k in range(1, snaps)]

    barrier = pltpu.get_barrier_semaphore()
    for peer in plane_peers + snap_peers:
        pl.semaphore_signal(barrier, inc=1, device_id=peer, device_id_type=MESH)
    features = terms_ref.shape[1]
    field_count, layers, columns, width = fields_ref.shape[1:]
    cells_rows = layers * columns
    square_rows = lax.broadcasted_iota(jnp.int32, (features, features), 0)
    square_columns = lax.broadcasted_iota(jnp.int32, (features, features), 1)

    def upright(row):
        return jnp.sum(jnp.where(square_rows == square_columns, row, 0.0), axis=1, keepdims=True)

    slot = lax.broadcasted_iota(jnp.int32, (features, 96), 1)
    base_of = lax.rem(slot, 32).astype(jnp.float32)
    chosen = [
        (upright(terms_ref[k : k + 1, :].astype(jnp.float32)) == base_of)
        .astype(jnp.float32)
        .astype(jnp.bfloat16)
        for k in range(3)
    ]
    choose = jnp.concatenate(chosen, axis=0)
    mix = upright(mix_ref[...])
    table = lax.broadcasted_iota(jnp.int32, weight_ref.shape, 1)
    scale = jnp.sum(
        jnp.where(table == ids_ref[0], weight_ref[...], 0.0), axis=1, keepdims=True
    )
    natural[28 * cells_rows :, :] = jnp.zeros((4 * cells_rows, width), jnp.float32)

    def put(field, kind, layer, tile):
        start = (field * 7 + kind) * cells_rows + layer * columns
        natural[start : start + columns, :] = tile

    def pair(center, ahead_one, behind_one, ahead_two, behind_two):
        first = 8.0 * (ahead_one - behind_one) - (ahead_two - behind_two)
        second = 16.0 * (ahead_one + behind_one) - (ahead_two + behind_two) - 30.0 * center
        return first * (1.0 / 12.0), second * (1.0 / 12.0)

    for f in range(field_count):
        for z in range(layers):
            tile = fields_ref[0, f, z]
            put(f, 0, z, tile)
            y_shifts = [pltpu.roll(tile, s % width, 1) for s in (-1, 1, -2, 2)]
            first, second = pair(tile, *y_shifts)
            put(f, 3, z, first)
            put(f, 6, z, second)

    pl.semaphore_wait(barrier, len(plane_peers) + len(snap_peers))

    copies = []
    for axis, index, count, halo, base in (
        ("slab", slab, slabs, halo_z, 0),
        ("sub", sub, subs, halo_x, 2),
    ):
        for side, move in ((0, 1), (1, count - 1))[: 1 if count == 2 else 2]:
            copy = pltpu.make_async_remote_copy(
                src_ref=fields_ref.at[0],
                dst_ref=halo.at[side],
                send_sem=halo_send.at[base + side],
                recv_sem=halo_recv.at[base + side],
                device_id={axis: lax.rem(index + move, count)},
                device_id_type=MESH,
            )
            copy.start()
            copies.append(copy)

    for copy in copies:
        copy.wait()

    z_low, z_high = 0, 0 if slabs == 2 else 1
    x_low, x_high = 0, 0 if subs == 2 else 1
    line = lax.broadcasted_iota(jnp.int32, (columns, width), 0)
    for f in range(field_count):
        column = [halo_z[z_low, f, z] for z in range(layers)]
        column += [fields_ref[0, f, z] for z in range(layers)]
        column += [halo_z[z_high, f, z] for z in range(layers)]
        for z in range(layers):
            tile = column[layers + z]
            at = layers + z
            first, second = pair(
                tile, column[at + 1], column[at - 1], column[at + 2], column[at - 2]
            )
            put(f, 1, z, first)
            put(f, 4, z, second)
            low, high = halo_x[x_low, f, z], halo_x[x_high, f, z]
            shifts = []
            for s in (-1, 1, -2, 2):
                turned = pltpu.roll(tile, s % columns, 0)
                other = pltpu.roll(high if s < 0 else low, s % columns, 0)
                inside = line < columns + s if s < 0 else line >= s
                shifts.append(jnp.where(inside, turned, other))
            first, second = pair(tile, *shifts)
            put(f, 2, z, first)
            put(f, 5, z, second)

    for start in range(0, cells_rows, 2):
        pieces = []
        for at in (start, start + 1):
            whole = natural[pl.ds(at, 32, stride=cells_rows), :]
            upper = whole.astype(jnp.bfloat16)
            rest = whole - upper.astype(jnp.float32)
            centre = rest.astype(jnp.bfloat16)
            lower = (rest - centre.astype(jnp.float32)).astype(jnp.bfloat16)
            pieces.append(jnp.concatenate([upper, centre, lower], axis=0))
        picked = jnp.dot(
            choose, jnp.concatenate(pieces, axis=1), preferred_element_type=jnp.float32
        )
        left, middle = picked[:features], picked[features : 2 * features]
        right = picked[2 * features :]
        feature_ref[:, start * width : (start + 2) * width] = (
            scale * left * (middle + mix * right)
        )

    feature_copy = pltpu.make_async_copy(feature_ref, feature_out, feature_done)
    feature_copy.start()
    everything = feature_ref[...]
    wide = gram_wide.shape[1]
    gram_wide[:, :features] = lax.dot_general(
        everything,
        everything,
        (((1,), (1,)), ((), ())),
        precision=HIGHEST,
        preferred_element_type=jnp.float32,
    )
    half = features // 2
    above = gram_wide[:half, :]
    below = gram_wide[half:, :]
    row = lax.broadcasted_iota(jnp.int32, (half, wide), 0)
    lane = lax.broadcasted_iota(jnp.int32, (half, wide), 1)
    corner = jnp.sum(jnp.where(lane == row + half, below, 0.0), axis=1, keepdims=True)
    packed = jnp.where(
        lane < half,
        jnp.where(lane >= row, above, pltpu.roll(below, wide - half, 1)),
        jnp.where(lane < features, above, corner),
    )
    rows = half // plane
    for k in range(plane):
        partial[k] = packed[k * rows : (k + 1) * rows, :]

    copies = []
    for k in range(1, plane):
        copy = pltpu.make_async_remote_copy(
            src_ref=partial.at[lax.rem(me + k, plane)],
            dst_ref=landed.at[k - 1],
            send_sem=plane_send.at[k - 1],
            recv_sem=plane_recv.at[k - 1],
            device_id=plane_peers[k - 1],
            device_id_type=MESH,
        )
        copy.start()
        copies.append(copy)
    block = partial[me]
    for k in range(1, plane):
        copies[k - 1].wait()
        block = block + landed[k - 1]
    snaps_sum[snap] = block

    copies = []
    for k in range(1, snaps):
        copy = pltpu.make_async_remote_copy(
            src_ref=snaps_sum.at[snap],
            dst_ref=snaps_sum.at[snap],
            send_sem=snap_send.at[k - 1],
            recv_sem=snap_recv.at[k - 1],
            device_id=snap_peers[k - 1],
            device_id_type=MESH,
        )
        copy.start()
        copies.append(copy)
    for copy in copies:
        copy.wait()
    block = snaps_sum[0]
    for k in range(1, snaps):
        block = block + snaps_sum[k]
    total[me] = block

    copies = []
    for k in range(1, plane):
        copy = pltpu.make_async_remote_copy(
            src_ref=total.at[me],
            dst_ref=total.at[me],
            send_sem=gather_send.at[k - 1],
            recv_sem=gather_recv.at[k - 1],
            device_id=plane_peers[k - 1],
            device_id_type=MESH,
        )
        copy.start()
        copies.append(copy)
    for copy in copies:
        copy.wait()
    for k in range(plane):
        packed_ref[k * rows : (k + 1) * rows, :] = total[k]
    feature_copy.wait()


def local(fields, snap_ids, snap_weight, product_terms, mix_weight):
    counts = tuple(lax.axis_size(axis) for axis in ("slab", "sub", "snap"))
    slabs, subs, snaps = counts
    plane = slabs * subs
    field_count, layers, columns, width = fields.shape[1:]
    features = product_terms.shape[0]
    cells = layers * columns * width
    half = features // 2
    rows = half // plane
    wide = features // 128 * 128 + 128
    f32 = jnp.float32
    in_vmem = pl.BlockSpec(memory_space=pltpu.VMEM)
    total_gram, values = pl.pallas_call(
        functools.partial(gram_kernel, counts),
        out_shape=(
            jax.ShapeDtypeStruct((half, wide), f32),
            jax.ShapeDtypeStruct((features, cells), f32),
        ),
        in_specs=[in_vmem, pl.BlockSpec(memory_space=pltpu.SMEM), in_vmem, in_vmem, in_vmem],
        out_specs=(in_vmem, pl.BlockSpec(memory_space=pl.ANY)),
        scratch_shapes=[
            pltpu.VMEM((features, cells), f32),
            pltpu.VMEM((features, wide), f32),
            pltpu.SemaphoreType.DMA,
            pltpu.VMEM((2,) + fields.shape[1:], f32),
            pltpu.VMEM((2,) + fields.shape[1:], f32),
            pltpu.VMEM((32 * layers * columns, width), f32),
            pltpu.VMEM((plane, rows, wide), f32),
            pltpu.VMEM((plane - 1, rows, wide), f32),
            pltpu.VMEM((snaps, rows, wide), f32),
            pltpu.VMEM((plane, rows, wide), f32),
            pltpu.SemaphoreType.DMA((4,)),
            pltpu.SemaphoreType.DMA((4,)),
            pltpu.SemaphoreType.DMA((plane - 1,)),
            pltpu.SemaphoreType.DMA((plane - 1,)),
            pltpu.SemaphoreType.DMA((snaps - 1,)),
            pltpu.SemaphoreType.DMA((snaps - 1,)),
            pltpu.SemaphoreType.DMA((plane - 1,)),
            pltpu.SemaphoreType.DMA((plane - 1,)),
        ],
        compiler_params=pltpu.CompilerParams(collective_id=0, has_side_effects=True),
    )(fields, snap_ids, snap_weight.reshape(1, -1), product_terms.T, mix_weight.reshape(1, -1))
    whitened, r_factor = pl.pallas_call(
        functools.partial(whiten_kernel, float(snaps * plane * cells)),
        out_shape=(
            jax.ShapeDtypeStruct((1, features, layers, columns, width), jnp.bfloat16),
            jax.ShapeDtypeStruct((features, features), f32),
        ),
        in_specs=[in_vmem, pl.BlockSpec(memory_space=pl.ANY)],
        out_specs=(in_vmem, in_vmem),
        scratch_shapes=[
            pltpu.VMEM((features, 2 * wide), f32),
            pltpu.VMEM((features * (cells // 128), 128), f32),
            pltpu.VMEM((features, cells), f32),
            pltpu.SemaphoreType.DMA,
        ],
    )(total_gram, values)
    return (whitened, r_factor)


def solution(mesh):
    return jax.shard_map(
        local,
        mesh=mesh,
        in_specs=(
            P(("groups", "snap"), None, "slab", "sub", None),
            P(("groups", "snap")),
            P(),
            P(),
            P(),
        ),
        out_specs=(P(("groups", "snap"), None, "slab", "sub", None), P("groups", None)),
        check_vma=False,
    )
```

```python
import functools

import jax
import jax.numpy as jnp
from jax import lax
from jax.experimental import pallas as pl
from jax.experimental.pallas import tpu as pltpu
from jax.sharding import PartitionSpec as P

ridge_value = 0.05
panel_rows = 32
HIGHEST = lax.Precision.HIGHEST
MESH = pl.DeviceIdType.MESH


def split(values, count):
    parts = []
    for _ in range(count):
        part = values.astype(jnp.bfloat16)
        parts.append(part)
        values = values - part.astype(jnp.float32)
    return parts


def row_of(tile, place):
    return jnp.broadcast_to(tile[place : place + 1, :], tile.shape)


def eliminate_group(groups, first, place):
    line = lax.broadcasted_iota(jnp.int32, (8, 128), 0)
    lane_tile, lane = place // 128, place % 128
    later = range(first, len(groups))
    spread = {
        (r, c): jnp.broadcast_to(
            groups[r][lane_tile][:, lane + c : lane + c + 1], (8, 128)
        )
        for r in later
        for c in range(8)
    }
    pivots = jnp.ones((8, 128), jnp.float32)
    factors = []
    for j in range(8):
        pivot = row_of(spread[first, j], j)
        pivots = jnp.where(line == j, pivot, pivots)
        inverse = 1.0 / pivot
        scaled = {r: spread[r, j] * inverse for r in later}
        scaled[first] = jnp.where(line > j, scaled[first], 0.0)
        factors.append(scaled)
        for c in range(j + 1, 8):
            head = row_of(spread[first, c], j)
            for r in later:
                spread[r, c] = spread[r, c] - scaled[r] * head
    for t in range(len(groups[first])):
        tile = groups[first][t]
        for j in range(8):
            head = row_of(tile, j)
            if j < 7:
                tile = tile - factors[j][first] * head
            for r in later:
                if r > first:
                    groups[r][t] = groups[r][t] - factors[j][r] * head
        groups[first][t] = tile
    return 1.0 / jnp.sqrt(pivots)


def eliminate(work, order):
    half = work.shape[1] // 2
    for start in range(0, order, panel_rows):
        stop = start + panel_rows
        low = start // 128 * 128
        high = half + (stop + 127) // 128 * 128
        tiles = (high - low) // 128
        groups = [
            [work[r : r + 8, low + 128 * t : low + 128 * t + 128] for t in range(tiles)]
            for r in range(start, stop, 8)
        ]
        scales = [
            eliminate_group(groups, g, start + 8 * g - low) for g in range(panel_rows // 8)
        ]
        rows = [
            jnp.concatenate([tile * scale for tile in group], axis=1)
            for group, scale in zip(groups, scales)
        ]
        panel = jnp.concatenate(rows, axis=0)
        work[start:stop, low:high] = panel
        if stop < order:
            sides = panel[:, : half - low].T[stop - low : order - low, :]
            a, b, c = split(sides, 3)
            d, e, f = split(panel, 3)
            left = jnp.concatenate([a, a, b, b, a, c], axis=1)
            right = jnp.concatenate([d, e, d, e, f, d], axis=0)
            work[stop:order, low:high] = work[stop:order, low:high] - jnp.dot(
                left, right, preferred_element_type=jnp.float32
            )


def whiten_kernel(
    cells_total, packed_ref, feature_in, white_ref, factor_ref, work, spread, feature_ref, done
):
    feature_copy = pltpu.make_async_copy(feature_in, feature_ref, done)
    feature_copy.start()
    order = factor_ref.shape[0]
    middle = packed_ref.shape[0]
    half = work.shape[1] // 2
    rows = lax.broadcasted_iota(jnp.int32, (order, order), 0)
    columns = lax.broadcasted_iota(jnp.int32, (order, order), 1)
    row = lax.broadcasted_iota(jnp.int32, (middle, 128), 0)
    lane = lax.broadcasted_iota(jnp.int32, (middle, 128), 1)
    left = packed_ref[:, :128]
    turned = jnp.concatenate([left, jnp.zeros((128 - middle, 128), jnp.float32)], axis=0).T
    turned = turned[:middle, :]
    work[:middle, :128] = jnp.where((lane >= row) | (lane >= middle), left, turned)
    work[:middle, 128:half] = jnp.where(lane + 128 < order, packed_ref[:, 128:], 0.0)
    corner = packed_ref[:, order : order + 1]
    lower = jnp.where(lane < row, left, jnp.where(lane > row, turned, corner))
    lower = jnp.where(lane < middle, lower, 0.0)
    lower = jnp.concatenate([lower, jnp.zeros((middle, half - 128), jnp.float32)], axis=1)
    work[middle:, :half] = pltpu.roll(lower, middle, 1)
    long_rows = lax.broadcasted_iota(jnp.int32, (order, half), 0)
    long_columns = lax.broadcasted_iota(jnp.int32, (order, half), 1)
    identity = (long_rows == long_columns).astype(jnp.float32)
    work[:, half:] = identity
    work[:, :half] = work[:, :half] * (1.0 / cells_total) + ridge_value * identity
    eliminate(work, order)
    factor_ref[...] = jnp.where(columns >= rows, work[:, :order], 0.0)
    inverse = jnp.where(columns <= rows, work[:, half : half + order], 0.0)
    upper, lower = split(inverse, 2)
    feature_copy.wait()
    tiles = feature_ref.shape[1] // 128
    for tile in range(0, tiles, 2):
        first, second = split(feature_ref[:, tile * 128 : tile * 128 + 256], 2)
        solved = (
            jnp.dot(upper, first, preferred_element_type=jnp.float32)
            + jnp.dot(upper, second, preferred_element_type=jnp.float32)
            + jnp.dot(lower, first, preferred_element_type=jnp.float32)
        )
        spread[pl.ds(tile, order, stride=tiles), :] = solved[:, :128]
        spread[pl.ds(tile + 1, order, stride=tiles), :] = solved[:, 128:]
    white_ref[...] = spread[...].reshape(white_ref.shape).astype(white_ref.dtype)


def plane_device(place, subs):
    return {"slab": lax.div(place, subs), "sub": lax.rem(place, subs)}


def gram_kernel(
    counts,
    fields_in,
    ids_ref,
    weight_in,
    terms_in,
    mix_in,
    packed_ref,
    feature_out,
    fields_ref,
    weight_ref,
    terms_ref,
    mix_ref,
    load_done,
    feature_ref,
    gram_wide,
    feature_done,
    halo_z,
    halo_x,
    natural,
    partial,
    landed,
    snaps_sum,
    total,
    halo_send,
    halo_recv,
    plane_send,
    plane_recv,
    snap_send,
    snap_recv,
    gather_send,
    gather_recv,
):
    slabs, subs, snaps = counts
    plane = slabs * subs
    slab, sub, snap = lax.axis_index("slab"), lax.axis_index("sub"), lax.axis_index("snap")
    me = slab * subs + sub
    plane_peers = [plane_device(lax.rem(me + k, plane), subs) for k in range(1, plane)]
    snap_peers = [{"snap": lax.rem(snap + k, snaps)} for k in range(1, snaps)]

    loads = [
        pltpu.make_async_copy(source, target, load_done.at[k])
        for k, (source, target) in enumerate(
            (
                (fields_in, fields_ref),
                (terms_in, terms_ref),
                (mix_in, mix_ref),
                (weight_in, weight_ref),
            )
        )
    ]
    for load in loads:
        load.start()
    barrier = pltpu.get_barrier_semaphore()
    for peer in plane_peers + snap_peers:
        pl.semaphore_signal(barrier, inc=1, device_id=peer, device_id_type=MESH)
    for load in loads:
        load.wait()
    features = terms_ref.shape[1]
    field_count, layers, columns, width = fields_ref.shape[1:]
    cells_rows = layers * columns
    square_rows = lax.broadcasted_iota(jnp.int32, (features, features), 0)
    square_columns = lax.broadcasted_iota(jnp.int32, (features, features), 1)

    def upright(row):
        return jnp.sum(jnp.where(square_rows == square_columns, row, 0.0), axis=1, keepdims=True)

    slot = lax.broadcasted_iota(jnp.int32, (features, 96), 1)
    base_of = lax.rem(slot, 32).astype(jnp.float32)
    chosen = [
        (upright(terms_ref[k : k + 1, :].astype(jnp.float32)) == base_of)
        .astype(jnp.float32)
        .astype(jnp.bfloat16)
        for k in range(3)
    ]
    choose = jnp.concatenate(chosen, axis=0)
    mix = upright(mix_ref[...])
    table = lax.broadcasted_iota(jnp.int32, weight_ref.shape, 1)
    scale = jnp.sum(
        jnp.where(table == ids_ref[0], weight_ref[...], 0.0), axis=1, keepdims=True
    )
    natural[28 * cells_rows :, :] = jnp.zeros((4 * cells_rows, width), jnp.float32)

    def put(field, kind, layer, tile):
        start = (field * 7 + kind) * cells_rows + layer * columns
        natural[start : start + columns, :] = tile

    def pair(center, ahead_one, behind_one, ahead_two, behind_two):
        first = 8.0 * (ahead_one - behind_one) - (ahead_two - behind_two)
        second = 16.0 * (ahead_one + behind_one) - (ahead_two + behind_two) - 30.0 * center
        return first * (1.0 / 12.0), second * (1.0 / 12.0)

    for f in range(field_count):
        for z in range(layers):
            tile = fields_ref[0, f, z]
            put(f, 0, z, tile)
            y_shifts = [pltpu.roll(tile, s % width, 1) for s in (-1, 1, -2, 2)]
            first, second = pair(tile, *y_shifts)
            put(f, 3, z, first)
            put(f, 6, z, second)

    pl.semaphore_wait(barrier, len(plane_peers) + len(snap_peers))

    copies = []
    for axis, index, count, halo, base in (
        ("slab", slab, slabs, halo_z, 0),
        ("sub", sub, subs, halo_x, 2),
    ):
        for side, move in ((0, 1), (1, count - 1))[: 1 if count == 2 else 2]:
            copy = pltpu.make_async_remote_copy(
                src_ref=fields_ref.at[0],
                dst_ref=halo.at[side],
                send_sem=halo_send.at[base + side],
                recv_sem=halo_recv.at[base + side],
                device_id={axis: lax.rem(index + move, count)},
                device_id_type=MESH,
            )
            copy.start()
            copies.append(copy)

    for copy in copies:
        copy.wait()

    z_low, z_high = 0, 0 if slabs == 2 else 1
    x_low, x_high = 0, 0 if subs == 2 else 1
    line = lax.broadcasted_iota(jnp.int32, (columns, width), 0)
    for f in range(field_count):
        column = [halo_z[z_low, f, z] for z in range(layers)]
        column += [fields_ref[0, f, z] for z in range(layers)]
        column += [halo_z[z_high, f, z] for z in range(layers)]
        for z in range(layers):
            tile = column[layers + z]
            at = layers + z
            first, second = pair(
                tile, column[at + 1], column[at - 1], column[at + 2], column[at - 2]
            )
            put(f, 1, z, first)
            put(f, 4, z, second)
            low, high = halo_x[x_low, f, z], halo_x[x_high, f, z]
            shifts = []
            for s in (-1, 1, -2, 2):
                turned = pltpu.roll(tile, s % columns, 0)
                other = pltpu.roll(high if s < 0 else low, s % columns, 0)
                inside = line < columns + s if s < 0 else line >= s
                shifts.append(jnp.where(inside, turned, other))
            first, second = pair(tile, *shifts)
            put(f, 2, z, first)
            put(f, 5, z, second)

    for start in range(0, cells_rows, 2):
        pieces = []
        for at in (start, start + 1):
            whole = natural[pl.ds(at, 32, stride=cells_rows), :]
            upper = whole.astype(jnp.bfloat16)
            rest = whole - upper.astype(jnp.float32)
            centre = rest.astype(jnp.bfloat16)
            lower = (rest - centre.astype(jnp.float32)).astype(jnp.bfloat16)
            pieces.append(jnp.concatenate([upper, centre, lower], axis=0))
        picked = jnp.dot(
            choose, jnp.concatenate(pieces, axis=1), preferred_element_type=jnp.float32
        )
        left, middle = picked[:features], picked[features : 2 * features]
        right = picked[2 * features :]
        feature_ref[:, start * width : (start + 2) * width] = (
            scale * left * (middle + mix * right)
        )

    feature_copy = pltpu.make_async_copy(feature_ref, feature_out, feature_done)
    feature_copy.start()
    everything = feature_ref[...]
    wide = gram_wide.shape[1]
    gram_wide[:, :features] = lax.dot_general(
        everything,
        everything,
        (((1,), (1,)), ((), ())),
        precision=HIGHEST,
        preferred_element_type=jnp.float32,
    )
    half = features // 2
    above = gram_wide[:half, :]
    below = gram_wide[half:, :]
    row = lax.broadcasted_iota(jnp.int32, (half, wide), 0)
    lane = lax.broadcasted_iota(jnp.int32, (half, wide), 1)
    corner = jnp.sum(jnp.where(lane == row + half, below, 0.0), axis=1, keepdims=True)
    packed = jnp.where(
        lane < half,
        jnp.where(lane >= row, above, pltpu.roll(below, wide - half, 1)),
        jnp.where(lane < features, above, corner),
    )
    rows = half // plane
    for k in range(plane):
        partial[k] = packed[k * rows : (k + 1) * rows, :]

    copies = []
    for k in range(1, plane):
        copy = pltpu.make_async_remote_copy(
            src_ref=partial.at[lax.rem(me + k, plane)],
            dst_ref=landed.at[k - 1],
            send_sem=plane_send.at[k - 1],
            recv_sem=plane_recv.at[k - 1],
            device_id=plane_peers[k - 1],
            device_id_type=MESH,
        )
        copy.start()
        copies.append(copy)
    block = partial[me]
    for k in range(1, plane):
        copies[k - 1].wait()
        block = block + landed[k - 1]
    snaps_sum[snap] = block

    copies = []
    for k in range(1, snaps):
        copy = pltpu.make_async_remote_copy(
            src_ref=snaps_sum.at[snap],
            dst_ref=snaps_sum.at[snap],
            send_sem=snap_send.at[k - 1],
            recv_sem=snap_recv.at[k - 1],
            device_id=snap_peers[k - 1],
            device_id_type=MESH,
        )
        copy.start()
        copies.append(copy)
    for copy in copies:
        copy.wait()
    block = snaps_sum[0]
    for k in range(1, snaps):
        block = block + snaps_sum[k]
    total[me] = block

    copies = []
    for k in range(1, plane):
        copy = pltpu.make_async_remote_copy(
            src_ref=total.at[me],
            dst_ref=total.at[me],
            send_sem=gather_send.at[k - 1],
            recv_sem=gather_recv.at[k - 1],
            device_id=plane_peers[k - 1],
            device_id_type=MESH,
        )
        copy.start()
        copies.append(copy)
    for copy in copies:
        copy.wait()
    for k in range(plane):
        packed_ref[k * rows : (k + 1) * rows, :] = total[k]
    feature_copy.wait()


def local(fields, snap_ids, snap_weight, product_terms, mix_weight):
    counts = tuple(lax.axis_size(axis) for axis in ("slab", "sub", "snap"))
    slabs, subs, snaps = counts
    plane = slabs * subs
    field_count, layers, columns, width = fields.shape[1:]
    features = product_terms.shape[0]
    cells = layers * columns * width
    half = features // 2
    rows = half // plane
    wide = features // 128 * 128 + 128
    f32 = jnp.float32
    in_vmem = pl.BlockSpec(memory_space=pltpu.VMEM)
    anywhere = pl.BlockSpec(memory_space=pl.ANY)
    total_gram, values = pl.pallas_call(
        functools.partial(gram_kernel, counts),
        out_shape=(
            pltpu.VMEM((half, wide), f32),
            jax.ShapeDtypeStruct((features, cells), f32),
        ),
        in_specs=[anywhere, pl.BlockSpec(memory_space=pltpu.SMEM)] + [anywhere] * 3,
        out_specs=(in_vmem, pl.BlockSpec(memory_space=pl.ANY)),
        scratch_shapes=[
            pltpu.VMEM(fields.shape, f32),
            pltpu.VMEM((1, snap_weight.shape[0]), f32),
            pltpu.VMEM((3, features), jnp.int32),
            pltpu.VMEM((1, features), f32),
            pltpu.SemaphoreType.DMA((4,)),
            pltpu.VMEM((features, cells), f32),
            pltpu.VMEM((features, wide), f32),
            pltpu.SemaphoreType.DMA,
            pltpu.VMEM((2,) + fields.shape[1:], f32),
            pltpu.VMEM((2,) + fields.shape[1:], f32),
            pltpu.VMEM((32 * layers * columns, width), f32),
            pltpu.VMEM((plane, rows, wide), f32),
            pltpu.VMEM((plane - 1, rows, wide), f32),
            pltpu.VMEM((snaps, rows, wide), f32),
            pltpu.VMEM((plane, rows, wide), f32),
            pltpu.SemaphoreType.DMA((4,)),
            pltpu.SemaphoreType.DMA((4,)),
            pltpu.SemaphoreType.DMA((plane - 1,)),
            pltpu.SemaphoreType.DMA((plane - 1,)),
            pltpu.SemaphoreType.DMA((snaps - 1,)),
            pltpu.SemaphoreType.DMA((snaps - 1,)),
            pltpu.SemaphoreType.DMA((plane - 1,)),
            pltpu.SemaphoreType.DMA((plane - 1,)),
        ],
        compiler_params=pltpu.CompilerParams(collective_id=0, has_side_effects=True),
    )(fields, snap_ids, snap_weight.reshape(1, -1), product_terms.T, mix_weight.reshape(1, -1))
    whitened, r_factor = pl.pallas_call(
        functools.partial(whiten_kernel, float(snaps * plane * cells)),
        out_shape=(
            jax.ShapeDtypeStruct((1, features, layers, columns, width), jnp.bfloat16),
            jax.ShapeDtypeStruct((features, features), f32),
        ),
        in_specs=[in_vmem, pl.BlockSpec(memory_space=pl.ANY)],
        out_specs=(in_vmem, in_vmem),
        scratch_shapes=[
            pltpu.VMEM((features, 2 * wide), f32),
            pltpu.VMEM((features * (cells // 128), 128), f32),
            pltpu.VMEM((features, cells), f32),
            pltpu.SemaphoreType.DMA,
        ],
        compiler_params=pltpu.CompilerParams(vmem_limit_bytes=24 * 1024 * 1024),
    )(pltpu.with_memory_space_constraint(total_gram, pltpu.VMEM), values)
    return (whitened, r_factor)


def solution(mesh):
    return jax.shard_map(
        local,
        mesh=mesh,
        in_specs=(
            P(("groups", "snap"), None, "slab", "sub", None),
            P(("groups", "snap")),
            P(),
            P(),
            P(),
        ),
        out_specs=(P(("groups", "snap"), None, "slab", "sub", None), P("groups", None)),
        check_vma=False,
    )
```
